32 devices in a mesh: tm: 4 (over y, x), aux: 4 (over z), pair: 2 (over core).
Axes of the slice: x: 2, y: 2, z: 4, core: 2. Of those that a mesh axis runs over, the one named last changes fastest.
Arguments:
- factors: bfloat16 [3072, 5120], P('aux', 'pair'), may hold values from -0.078125 to 0.078125
- panel_factors: bfloat16 [256, 5120], P('aux', 'pair'), may hold values from -6 to 6
- time_weights: float32 [12, 5120], P('tm', 'pair'), may hold values from 0.2 to 2
- tile_mask: int32 [24, 40], P('aux', 'pair'), may hold values 0 or 1
- forward_table: float32 [12, 12], replicated, may hold values from -0.5 to 0.5
- screening: float32 [12, 256, 256], P('tm', 'aux'), may hold values from -0.375 to 0.375
- back_table: float32 [12, 12], replicated, may hold values from -0.5 to 0.5
Outputs:
- sigma: float32 [12, 5120], P('tm', 'pair')
The draws below stay inside these ranges and needn't reach their ends.
All inputs are finite; a program needn't handle non-finite values. No bound on the sum of `tile_mask` on one device may be relied on, other than what follows from the above.
Results may differ from the reference program's by a relative error of at most 0.0003.
Values may be sent and summed in bfloat16 or wider, within the bound.
No kernel may reach another device: no remote copies, remote signals or barrier semaphores. Data moves between devices by JAX's collectives and lax.ppermute only.
A program may use at most 64 MiB of HBM per device.

```python
import math
import jax
import jax.numpy as jnp
from jax import lax

TILE = 128
NP = 256
NT = 12
NW = 12
NAUX = 3072
NPAIR = 5120


def touch_ends(result, key, low, top_value):
    index_at = [jax.random.randint(jax.random.fold_in(key, axis), (), 0, length) for axis, length in enumerate(result.shape)]
    longest = result.shape.index(max(result.shape))
    beside = index_at[:longest] + [(index_at[longest] + 1) % result.shape[longest]] + index_at[longest + 1:]
    return result.at[tuple(index_at)].set(low).at[tuple(beside)].set(top_value)


def block_scale(key, shape, shards, least, high):
    factor_of = 1.0
    for dim, blocks in shards:
        draws = jax.random.uniform(jax.random.fold_in(jax.random.fold_in(key, 6), dim), (blocks,), jnp.float32, least / len(shards), high / len(shards))
        factor_of = factor_of * jnp.repeat(jnp.exp(draws), shape[dim] // blocks).reshape((-1,) + (1,) * (len(shape) - 1 - dim))
    return factor_of


def bell_draw(stream_key, dims, width, bound, split=(), kind=jnp.bfloat16):
    factor_of = block_scale(stream_key, dims, split, -0.22, 0.18) if split else 1.0
    drawn = jax.random.normal(stream_key, dims, jnp.float32) * width * factor_of
    return jnp.minimum(jnp.maximum(drawn, -bound), bound).astype(kind)


def setup_inputs(seed: int = 0) -> dict:
    splits = jax.random.split(jax.random.key(seed), 8)
    factors = bell_draw(splits[0], (NAUX, NPAIR), NPAIR ** -0.5, 0.078125, ((0, 4), (1, 2)))
    panel_factors = bell_draw(splits[1], (NP, NPAIR), 1.0, 6.0, ((0, 4), (1, 2)))
    time_weights = jnp.clip(jnp.exp(math.log(2.0) - 2.3025851 * jax.random.uniform(splits[2], (NT, NPAIR), jnp.float32) ** block_scale(splits[2], (NT, NPAIR), ((0, 4), (1, 2)), -0.2, 0.2)), 0.2, 2.0)
    tile_mask = touch_ends((jax.random.randint(splits[3], (NAUX // TILE, NPAIR // TILE), 0, 4) < 3).astype(jnp.int32), jax.random.fold_in(splits[3], 1), 0, 1)
    forward_table = jnp.clip(jax.random.uniform(splits[4], (NW, NT), jnp.float32, -0.5, 0.5), -0.5, 0.5)
    screening = bell_draw(splits[5], (NW, NP, NP), NP ** -0.5, 0.375, ((0, 4), (1, 4)), jnp.float32)
    back_table = jnp.clip(jax.random.uniform(splits[6], (NT, NW), jnp.float32, -0.5, 0.5), -0.5, 0.5)
    return {"factors": factors, "panel_factors": panel_factors, "time_weights": time_weights, "tile_mask": tile_mask, "forward_table": forward_table, "screening": screening, "back_table": back_table}


def expand_tiles(tile_mask):
    tile_rows, tile_cols = tile_mask.shape
    spread = jnp.broadcast_to(tile_mask[:, None, :, None], (tile_rows, TILE, tile_cols, TILE))
    return spread.reshape(tile_rows * TILE, tile_cols * TILE)


def reference(factors, panel_factors, time_weights, tile_mask, forward_table, screening, back_table):
    highest = lax.Precision.HIGHEST
    masked = factors.astype(jnp.float32) * expand_tiles(tile_mask).astype(jnp.float32)
    panel_wide = panel_factors.astype(jnp.float32)
    scaled = panel_wide[None, :, :] * time_weights[:, None, :]

    def polar_one(scaled_time):
        return jnp.dot(scaled_time, masked.T, precision=highest)

    polar_time = lax.map(polar_one, scaled)
    polar_freq = jnp.einsum("wt,tpq->wpq", forward_table, polar_time, precision=highest)
    screened = jnp.einsum("wpr,wrq->wpq", screening, polar_freq, precision=highest)
    retimed = jnp.einsum("tw,wpq->tpq", back_table, screened, precision=highest)

    def contract_one(retimed_time):
        return jnp.dot(retimed_time, masked, precision=highest)

    contracted = lax.map(contract_one, retimed)
    sigma = jnp.sum(panel_wide[None, :, :] * contracted, axis=1) * (NP ** -0.5)
    return sigma
```

```python
import functools

import jax
import jax.numpy as jnp
from jax import lax
from jax.experimental import pallas as pl
from jax.experimental.pallas import tpu as pltpu
from jax.sharding import PartitionSpec as P

TILE = 128
F8 = jnp.float8_e4m3fn
BF = jnp.bfloat16
F32 = jnp.float32
TOP = 256.0
TINY = 1e-30
SMEM = pltpu.MemorySpace.SMEM
VMEM = pltpu.MemorySpace.VMEM


def dot_nt(a, b):
    return lax.dot_general(a, b, (((1,), (1,)), ((), ())), preferred_element_type=F32)


def dot_nn(a, b):
    return lax.dot_general(a, b, (((1,), (0,)), ((), ())), preferred_element_type=F32)


def swap_with(value, axis, step, size):
    return lax.ppermute(value, axis, [(at, at ^ step) for at in range(size)])


def cost(flops, nbytes):
    return pl.CostEstimate(flops=int(flops), bytes_accessed=int(nbytes), transcendentals=0)


def mask_kernel(tile_ref, factors_ref, wide_ref, narrow_ref, scale_ref):
    rows, cols = factors_ref.shape
    top = jnp.zeros((TILE, TILE), F32)
    for col in range(0, cols, TILE):
        for row in range(0, rows, TILE):
            top = jnp.maximum(top, jnp.abs(factors_ref[row : row + TILE, col : col + TILE].astype(F32)))
    scale = TOP / jnp.maximum(jnp.max(top), TINY)
    scale_ref[0] = 1.0 / scale
    for col in range(0, cols, TILE):
        for row in range(0, rows, TILE):
            keep = tile_ref[row // TILE, col // TILE].astype(F32)
            block = factors_ref[row : row + TILE, col : col + TILE].astype(F32) * keep
            wide_ref[row : row + TILE, col : col + TILE] = block.astype(BF)
            narrow_ref[row : row + TILE, col : col + TILE] = (block * scale).astype(F8)


def mask_factors(tile_mask, factors):
    vmem = pl.BlockSpec(memory_space=VMEM)
    smem = pl.BlockSpec(memory_space=SMEM)
    return pl.pallas_call(
        mask_kernel,
        name="mask",
        in_specs=[smem, vmem],
        out_specs=[vmem, vmem, smem],
        out_shape=[
            jax.ShapeDtypeStruct(factors.shape, BF),
            jax.ShapeDtypeStruct(factors.shape, F8),
            jax.ShapeDtypeStruct((1,), F32),
        ],
        compiler_params=pltpu.CompilerParams(vmem_limit_bytes=24 << 20),
        cost_estimate=cost(4 * factors.size, 5 * factors.size),
    )(tile_mask, factors)


def combine_kernel(factor, count, at_ref, table_ref, *refs):
    blocks, out_ref = refs[:-1], refs[-1]
    me = at_ref[0]
    size = blocks[0].shape[0]
    total = [None] * count
    for step, block_ref in enumerate(blocks):
        first = (me ^ step) * size
        for line in range(size):
            values = block_ref[line : line + 1, :]
            for row in range(count):
                term = values * table_ref[me * count + row, first + line]
                total[row] = term if total[row] is None else total[row] + term
    for row in range(count):
        out_ref[row : row + 1, :] = total[row] * factor if factor != 1.0 else total[row]


def combine(at, table, blocks, count, factor, name):
    vmem = pl.BlockSpec(memory_space=VMEM)
    smem = pl.BlockSpec(memory_space=SMEM)
    return pl.pallas_call(
        functools.partial(combine_kernel, factor, count),
        name=name,
        in_specs=[smem, smem] + [vmem] * len(blocks),
        out_specs=vmem,
        out_shape=jax.ShapeDtypeStruct((count, blocks[0].shape[1]), F32),
        compiler_params=pltpu.CompilerParams(vmem_limit_bytes=8 << 20),
        cost_estimate=cost(100 * blocks[0].size, 4 * blocks[0].size * (len(blocks) + 1)),
    )(at, table, *blocks)


def polar_kernel(n_pieces, scale_ref, weights_ref, *refs):
    pieces = refs[:n_pieces]
    wide_ref, narrow_ref, out_ref, high, low = refs[n_pieces:]
    lines = weights_ref.shape[0]
    rows = high.shape[0] // lines

    @pl.when(pl.program_id(0) == 0)
    def _():
        out_ref[...] = jnp.zeros_like(out_ref)

    unscale = scale_ref[0]
    for line in range(lines):
        weight = weights_ref[line : line + 1, :]
        bound = jnp.max(jnp.abs(weight), axis=1, keepdims=True) * (1.0 / 256.0)
        backs = []
        at = line * rows
        for piece_ref in pieces:
            step = 32
            for start in range(0, piece_ref.shape[0], step):
                value = piece_ref[start : start + step, :].astype(F32)
                top = jnp.maximum(jnp.max(jnp.abs(value), axis=1, keepdims=True) * bound, TINY)
                back = top * (1.0 / TOP)
                value = value * weight
                rounded = value.astype(BF)
                high[at : at + step, :] = rounded
                low[at : at + step, :] = ((value - rounded.astype(F32)) * (1.0 / back)).astype(F8)
                backs.append(back * unscale)
                at += step
        span = slice(line * rows, (line + 1) * rows)
        back = jnp.concatenate(backs, axis=0)
        out_ref[span, :] += dot_nt(high[span, :], wide_ref[...]) + dot_nt(low[span, :], narrow_ref[...]) * back


def polar(scale, weights, pieces, wide, narrow, name, chunk=512):
    lines, depth = weights.shape
    rows = lines * sum(piece.shape[0] for piece in pieces)
    aux = wide.shape[0]
    part = lambda n: pl.BlockSpec((n, chunk), lambda k: (0, k))
    return pl.pallas_call(
        functools.partial(polar_kernel, len(pieces)),
        name=name,
        grid=(depth // chunk,),
        in_specs=[pl.BlockSpec(memory_space=SMEM), part(lines)]
        + [part(piece.shape[0]) for piece in pieces]
        + [part(aux), part(aux)],
        out_specs=pl.BlockSpec((rows, aux), lambda k: (0, 0)),
        out_shape=jax.ShapeDtypeStruct((rows, aux), F32),
        scratch_shapes=[pltpu.VMEM((rows, chunk), BF), pltpu.VMEM((rows, chunk), F8)],
        compiler_params=pltpu.CompilerParams(vmem_limit_bytes=24 << 20),
        cost_estimate=cost(3 * rows * aux * depth, 3 * aux * depth + 4 * rows * aux),
    )(scale, weights, *pieces, wide, narrow)


def split_rows(mine, other, high, low, back):
    step = 32
    for start in range(0, mine.shape[0], step):
        span = slice(start, start + step)
        value = mine[span, :] + other[span, :]
        rounded = value.astype(BF)
        rest = value - rounded.astype(F32)
        top = jnp.maximum(jnp.max(jnp.abs(rest), axis=1, keepdims=True), TINY) * (1.0 / TOP)
        high[span, :] = rounded
        low[span, :] = (rest * (1.0 / top)).astype(F8)
        back[span, :] = jnp.broadcast_to(top, (step, back.shape[1]))


def spread_kernel(scale_ref, mine_ref, other_ref, wide_ref, narrow_ref, out_ref, high, low, back):
    @pl.when(pl.program_id(0) == 0)
    def _():
        split_rows(mine_ref, other_ref, high, low, back)

    unscale = back[:, 0:1] * scale_ref[0]
    out_ref[...] = dot_nn(high[...], wide_ref[...]) + dot_nn(low[...], narrow_ref[...]) * unscale


def spread(scale, mine, other, wide, narrow, name, chunk=512):
    rows, aux = mine.shape
    depth = wide.shape[1]
    part = lambda n: pl.BlockSpec((n, chunk), lambda k: (0, k))
    whole = lambda shape: pl.BlockSpec(shape, lambda k: (0, 0))
    return pl.pallas_call(
        spread_kernel,
        name=name,
        grid=(depth // chunk,),
        in_specs=[pl.BlockSpec(memory_space=SMEM), whole((rows, aux)), whole((rows, aux)), part(aux), part(aux)],
        out_specs=part(rows),
        out_shape=jax.ShapeDtypeStruct((rows, depth), F32),
        scratch_shapes=[
            pltpu.VMEM((rows, aux), BF),
            pltpu.VMEM((rows, aux), F8),
            pltpu.VMEM((rows, TILE), F32),
        ],
        compiler_params=pltpu.CompilerParams(vmem_limit_bytes=24 << 20),
        cost_estimate=cost(3 * rows * aux * depth, 3 * aux * depth + 4 * rows * (aux + depth)),
    )(scale, mine, other, wide, narrow)


def close_kernel(layout, groups, n_screen, at_ref, scale_ref, mine_ref, other_ref, wide_ref, narrow_ref, *refs):
    pieces = refs[: len(layout)]
    screens = refs[len(layout) : len(layout) + n_screen]
    done = refs[len(layout) + n_screen : len(layout) + n_screen + len(groups) - 1]
    out_ref, high, low, back, square, turned, rest, panel, folded, last = refs[len(layout) + n_screen + len(groups) - 1 :]
    lines, total = square.shape[0], square.shape[1]

    @pl.when(pl.program_id(0) == 0)
    def _():
        split_rows(mine_ref, other_ref, high, low, back)
        for line in range(lines):
            for which, screen_ref in enumerate(screens):
                size = screen_ref.shape[1]
                first = pl.multiple_of(at_ref[which] * size, size)
                square[line, pl.ds(first, size), :] = screen_ref[line]
            flipped = square[line].T
            rounded = flipped.astype(BF)
            turned[line] = rounded
            rest[line] = (flipped - rounded.astype(F32)).astype(BF)

    for piece_ref, (parts, n_rows) in zip(pieces, layout):
        for part, slot in enumerate(parts):
            first = pl.multiple_of(at_ref[slot], 16)
            panel[pl.ds(first, n_rows), :] = piece_ref[part * n_rows : (part + 1) * n_rows, :]
    unscale = back[:, 0:1] * scale_ref[0]
    last[...] = dot_nn(high[...], wide_ref[...]) + dot_nn(low[...], narrow_ref[...]) * unscale
    for line in range(lines):
        folded[...] = dot_nn(turned[line], panel[...]) + dot_nn(rest[line], panel[...])
        acc = jnp.zeros((8, last.shape[1]), F32)
        for number, group in enumerate(groups):
            block = done[number] if number < len(done) else last
            rows = block.shape[0] // lines
            at = line * rows
            for which in group:
                parts, n_rows = layout[which]
                for slot in parts:
                    first = at_ref[slot]
                    for row in range(0, n_rows, 8):
                        screened = folded[pl.ds(pl.multiple_of(first + row, 8), 8), :]
                        acc += screened * block[at : at + 8, :]
                        at += 8
        out_ref[line : line + 1, :] = jnp.sum(acc, axis=0, keepdims=True)


def close(at, scale, mine, other, wide, narrow, layout, groups, pieces, screens, done, chunk=512):
    rows, aux = mine.shape
    depth = wide.shape[1]
    lines, total = screens[0].shape[0], screens[0].shape[2]
    part = lambda n: pl.BlockSpec((n, chunk), lambda k: (0, k))
    whole = lambda shape: pl.BlockSpec(shape, lambda k: (0,) * len(shape))
    smem = pl.BlockSpec(memory_space=SMEM)
    return pl.pallas_call(
        functools.partial(close_kernel, layout, groups, len(screens)),
        name="close",
        grid=(depth // chunk,),
        in_specs=[smem, smem, whole((rows, aux)), whole((rows, aux)), part(aux), part(aux)]
        + [part(piece.shape[0]) for piece in pieces]
        + [whole(screen.shape) for screen in screens]
        + [part(block.shape[0]) for block in done],
        out_specs=part(lines),
        out_shape=jax.ShapeDtypeStruct((lines, depth), F32),
        scratch_shapes=[
            pltpu.VMEM((rows, aux), BF),
            pltpu.VMEM((rows, aux), F8),
            pltpu.VMEM((rows, TILE), F32),
            pltpu.VMEM((lines, total, total), F32),
            pltpu.VMEM((lines, total, total), BF),
            pltpu.VMEM((lines, total, total), BF),
            pltpu.VMEM((total, chunk), BF),
            pltpu.VMEM((total, chunk), F32),
            pltpu.VMEM((rows, chunk), F32),
        ],
        compiler_params=pltpu.CompilerParams(vmem_limit_bytes=40 << 20),
        cost_estimate=cost(3 * rows * aux * depth + 4 * lines * total * total * depth, 3 * aux * depth + 4 * lines * total * depth),
    )(at, scale, mine, other, wide, narrow, *pieces, *screens, *done)


def body(n_tm, n_aux, factors, panel, weights, tile_mask, forward_table, screening, back_table):
    tm, aux = lax.axis_index("tm"), lax.axis_index("aux")
    block, count = panel.shape[0], screening.shape[0]
    total = block * n_aux
    at_tm = jnp.stack([tm, aux])
    wide, narrow, scale = mask_factors(tile_mask, factors)
    all_weights = [weights] + [swap_with(weights, "tm", step, n_tm) for step in range(1, n_tm)]
    quarter = block // n_tm
    if n_aux == 4 and n_tm == 4 and quarter % 16 == 0:
        near = swap_with(panel, "aux", 1, n_aux)
        mine = lax.dynamic_slice_in_dim(panel, tm * quarter, quarter, 0)
        far = jnp.concatenate([swap_with(mine, "aux", step, n_aux) for step in (2, 3)], axis=0)
        fars = [far] + [swap_with(far, "tm", step, n_tm) for step in (1, 2, 3)]
        pieces = [panel, near] + fars
        slots = [aux ^ step for step in range(n_aux)]
        layout = []
        for step in (0, 1):
            layout.append(((len(slots),), block))
            slots.append((aux ^ step) * block)
        for step in range(n_tm):
            layout.append(((len(slots), len(slots) + 1), quarter))
            slots += [(aux ^ other) * block + (tm ^ step) * quarter for other in (2, 3)]
        groups = [[0], [1, 2], [3, 4, 5]]
        screens = [screening] + [swap_with(screening, "aux", step, n_aux) for step in range(1, n_aux)]
    else:
        full = lax.all_gather(panel, "aux", axis=0, tiled=True)
        cuts = [0, total // 4, total * 5 // 8, total]
        pieces = [full[low:high] for low, high in zip(cuts, cuts[1:])]
        slots = [jnp.zeros_like(tm)] + [jnp.full_like(tm, low) for low in cuts[:-1]]
        layout = [((1 + n,), high - low) for n, (low, high) in enumerate(zip(cuts, cuts[1:]))]
        groups = [[0], [1], [2]]
        screens = [lax.all_gather(screening, "aux", axis=1, tiled=True)]
    at = jnp.stack(slots)
    line_weights = combine(at_tm, forward_table, all_weights, count, 1.0, "weights")
    polars = []
    for number, group in enumerate(groups):
        own = polar(scale, line_weights, [pieces[which] for which in group], wide, narrow, f"polar{number}")
        polars.append((own, swap_with(own, "pair", 1, 2)))
    done = [spread(scale, *polars[n], wide, narrow, f"spread{n}") for n in range(len(groups) - 1)]
    value = close(at, scale, *polars[-1], wide, narrow, tuple(layout), groups, pieces, screens, done)
    if n_aux <= 4:
        value = value + sum(swap_with(value, "aux", step, n_aux) for step in range(1, n_aux))
    else:
        value = lax.psum(value, "aux")
    values = [value] + [swap_with(value, "tm", step, n_tm) for step in range(1, n_tm)]
    return combine(at_tm, back_table, values, weights.shape[0], total ** (-0.5), "sigma")


def solution(mesh):
    placed = (
        P("aux", "pair"),
        P("aux", "pair"),
        P("tm", "pair"),
        P("aux", "pair"),
        P(),
        P("tm", "aux", None),
        P(),
    )
    step = functools.partial(body, mesh.shape["tm"], mesh.shape["aux"])
    return jax.shard_map(step, mesh=mesh, in_specs=placed, out_specs=P("tm", "pair"), check_vma=False)
```
